128 devices in a mesh: ctx: 16 (over y, x), head: 8 (over z, core).
Axes of the slice: x: 4, y: 4, z: 4, core: 2. Of those that a mesh axis runs over, the one named last changes fastest.
Arguments:
- queries: bfloat16 [16384, 40, 128], P('ctx', 'head'), may hold values from -6 to 6
- key_rows: bfloat16 [16384, 40, 128], P('ctx', 'head'), may hold values from -0.5390625 to 0.5390625
- value_rows: bfloat16 [16384, 40, 128], P('ctx', 'head'), may hold values from -6 to 6
- level_weight: float32 [16384, 40, 16], P('ctx', 'head'), may hold values from 0.001 to 2.5, as said below
- norm_gain: float32 [40, 128], P('head'), may hold values from 0.25 to 1.75
- out_weight: bfloat16 [5120, 5120], P('head'), may hold values from -0.078125 to 0.078125
Outputs:
- mixed: bfloat16 [16384, 5120], P(('ctx', 'head'))
The draws below stay inside these ranges and needn't reach their ends.
Inputs may be any that keep to these rules, and one draw needn't show every extreme that they name: `level_weight`: positive level weights.
All inputs are finite; a program needn't handle non-finite values.
Results may differ from the reference program's by a relative error of at most 0.02.
Values may be sent and summed in bfloat16 or wider, within the bound.
No kernel may reach another device: no remote copies, remote signals or barrier semaphores. Data moves between devices by JAX's collectives and lax.ppermute only.
A program may use at most 128 MiB of HBM per device.

```python
import math
import jax
import jax.numpy as jnp
from jax import lax

D = 5120
HEADS = 40
DH = 128
CH = 128
LEVELS = 16
TOKENS = 16384
N_HEAD = 8


def draw_level_weight(key, part):
    full_shape = (TOKENS, HEADS, LEVELS)
    base_draw = jnp.exp(jax.random.uniform(key, full_shape, jnp.float32, math.log(0.25), math.log(2.5)))
    level_ids = jnp.arange(LEVELS, dtype=jnp.float32)
    shrink = jnp.exp2(-0.5 * jnp.maximum(level_ids - 1.0, 0.0))
    return base_draw * shrink[None, None, :]


def level_of(key, extent, shards, smallest, top_value):
    level, own = 1.0, jax.random.fold_in(key, 6)
    for dim, blocks in shards:
        steps = jnp.exp(jax.random.uniform(jax.random.fold_in(own, dim), (blocks,), jnp.float32, smallest / len(shards), top_value / len(shards)))
        level = level * jnp.repeat(steps, extent[dim] // blocks).reshape([-1 if axis == dim else 1 for axis in range(len(extent))])
    return level


def centred(own_key, extent, scale, reach, split=(), kind=jnp.bfloat16):
    gain = level_of(own_key, extent, split, -0.22, 0.18) if split else 1.0
    array = jax.random.normal(own_key, extent, jnp.float32) * scale * gain
    return jnp.minimum(jnp.maximum(array, -reach), reach).astype(kind)


def setup_inputs(seed: int = 0) -> dict:
    key_of = jax.random.split(jax.random.key(seed), 7)
    queries = centred(key_of[0], (TOKENS, HEADS, DH), 1.0, 6.0, ((0, 16), (1, 8)))
    key_rows = centred(key_of[1], (TOKENS, HEADS, DH), 0.09, 0.5390625, ((0, 16), (1, 8)))
    value_rows = centred(key_of[2], (TOKENS, HEADS, DH), 1.0, 6.0, ((0, 16), (1, 8)))
    level_weight = draw_level_weight(jax.random.fold_in(key_of[6], 71), 0)
    norm_gain = jnp.clip(1.0 + 0.15 * jax.random.normal(key_of[4], (HEADS, DH), jnp.float32), 0.25, 1.75)
    out_weight = centred(key_of[5], (HEADS * DH, D), (HEADS * DH) ** -0.5, 0.078125, ((0, 8),))
    return dict(queries=queries, key_rows=key_rows, value_rows=value_rows, level_weight=level_weight, norm_gain=norm_gain, out_weight=out_weight)


def level_table(stretch_len, level_count):
    position = jnp.arange(stretch_len, dtype=jnp.int32)
    xor_dist = jnp.bitwise_xor(position[:, None], position[None, :])
    level_ids = jnp.zeros((stretch_len, stretch_len), jnp.int32)
    for bit_idx in range(stretch_len.bit_length() - 1):
        level_ids = level_ids + (xor_dist >= 1 << bit_idx).astype(jnp.int32)
    level_onehot = (level_ids[:, :, None] == jnp.arange(level_count, dtype=jnp.int32)[None, None, :]).astype(jnp.float32)
    causal_keep = (position[:, None] >= position[None, :]).astype(jnp.float32)
    return level_onehot * causal_keep[:, :, None]

def stretch_local(queries, key_rows, value_rows, level_weight, stretch_len):
    tok_count, head_count, head_width = queries.shape
    level_count = level_weight.shape[2]
    stretch_count = tok_count // stretch_len
    q_stretches = queries.reshape(stretch_count, stretch_len, head_count, head_width).astype(jnp.float32)
    k_stretches = key_rows.reshape(stretch_count, stretch_len, head_count, head_width).astype(jnp.float32)
    v_stretches = value_rows.reshape(stretch_count, stretch_len, head_count, head_width).astype(jnp.float32)
    w_stretches = level_weight.reshape(stretch_count, stretch_len, head_count, level_count)
    scores = jnp.einsum('cthd,cshd->chts', q_stretches, k_stretches, precision=lax.Precision.HIGHEST)
    mix_weights = jnp.einsum('cthl,tsl->chts', w_stretches, level_table(stretch_len, level_count), precision=lax.Precision.HIGHEST)
    mixed_probs = lax.optimization_barrier((scores * mix_weights).astype(jnp.bfloat16)).astype(jnp.float32)
    near = jnp.einsum('chts,cshd->cthd', mixed_probs, v_stretches, precision=lax.Precision.HIGHEST)
    return near.reshape(tok_count, head_count, head_width)

def stretch_tree(queries, key_rows, value_rows, level_weight, stretch_len, first_level):
    tok_count, head_count, head_width = queries.shape
    stretch_count = tok_count // stretch_len
    q_stretches = queries.reshape(stretch_count, stretch_len, head_count, head_width).astype(jnp.float32)
    k_stretches = key_rows.reshape(stretch_count, stretch_len, head_count, head_width).astype(jnp.float32)
    v_stretches = value_rows.reshape(stretch_count, stretch_len, head_count, head_width).astype(jnp.float32)
    states = jnp.einsum('cshd,cshe->chde', k_stretches, v_stretches, precision=lax.Precision.HIGHEST)
    result = jnp.zeros((stretch_count, stretch_len, head_count, head_width), jnp.float32)
    span_len = 1
    level_step = 0
    while span_len < stretch_count:
        groups = stretch_count // (2 * span_len)
        left_sum = states.reshape(groups, 2, span_len, head_count, head_width, head_width)[:, 0].sum(axis=1)
        left_sum = lax.optimization_barrier(left_sum.astype(jnp.bfloat16)).astype(jnp.float32)
        upper_q = q_stretches.reshape(groups, 2, span_len, stretch_len, head_count, head_width)[:, 1]
        readout = jnp.einsum('gsthd,ghde->gsthe', upper_q, left_sum, precision=lax.Precision.HIGHEST)
        weights = level_weight.reshape(groups, 2, span_len, stretch_len, head_count, -1)[:, 1, :, :, :, first_level + level_step]
        filled = jnp.stack([jnp.zeros_like(readout), readout * weights[..., None]], axis=1)
        result = result + filled.reshape(stretch_count, stretch_len, head_count, head_width)
        span_len = span_len * 2
        level_step = level_step + 1
    return result.reshape(tok_count, head_count, head_width)

def reference(queries, key_rows, value_rows, level_weight, norm_gain, out_weight):
    first_level = CH.bit_length()

    def one_head(items):
        q_head, k_head, v_head, w_head = items
        q_head = q_head[:, None, :]
        k_head = k_head[:, None, :]
        v_head = v_head[:, None, :]
        w_head = w_head[:, None, :]
        near = stretch_local(q_head, k_head, v_head, w_head, CH)
        far = stretch_tree(q_head, k_head, v_head, w_head, CH, first_level)
        return (near + far)[:, 0, :]
    by_head = (jnp.transpose(queries, (1, 0, 2)), jnp.transpose(key_rows, (1, 0, 2)), jnp.transpose(value_rows, (1, 0, 2)), jnp.transpose(level_weight, (1, 0, 2)))
    attended = lax.map(one_head, by_head)
    mean_sq = lax.optimization_barrier(jnp.mean(attended * attended, axis=2, keepdims=True))
    normed = (attended * lax.rsqrt(mean_sq + 1e-06) * norm_gain[:, None, :]).astype(jnp.bfloat16)
    normed = jnp.transpose(normed, (1, 0, 2)).reshape(TOKENS, HEADS * DH)
    group_width = HEADS // N_HEAD * DH
    group_rows = normed.reshape(TOKENS, N_HEAD, group_width).transpose(1, 0, 2)
    group_weight = out_weight.reshape(N_HEAD, group_width, D)

    def add_group(running, pair):
        rows_in, weight_in = pair
        product = jnp.dot(rows_in.astype(jnp.float32), weight_in.astype(jnp.float32), precision=lax.Precision.HIGHEST)
        product = lax.optimization_barrier(product.astype(jnp.bfloat16)).astype(jnp.float32)
        return (running + product, None)
    summed, _ = lax.scan(add_group, jnp.zeros((TOKENS, D), jnp.float32), (group_rows, group_weight))
    return summed.astype(jnp.bfloat16)
```

```python
import jax
import jax.numpy as jnp
from jax import lax
from jax.experimental import pallas as pl
from jax.experimental.pallas import tpu as pltpu
from jax.sharding import PartitionSpec as P

CH = 128
F32 = jnp.float32
BF16 = jnp.bfloat16


def dot00(a, b):
    return lax.dot_general(a, b, (((0,), (0,)), ((), ())), preferred_element_type=F32)


def dot11(a, b):
    return lax.dot_general(a, b, (((1,), (1,)), ((), ())), preferred_element_type=F32)


def cost(flops, byte_count):
    return pl.CostEstimate(flops=flops, bytes_accessed=byte_count, transcendentals=0)


def state_body(k_ref, v_ref, out_ref):
    out_ref[0] = dot00(v_ref[0], k_ref[0])


def block_states(keys, values):
    heads, toks, dh = keys.shape
    spec = pl.BlockSpec((1, toks, dh), lambda h: (h, 0, 0))
    return pl.pallas_call(
        state_body,
        grid=(heads,),
        in_specs=[spec, spec],
        out_specs=pl.BlockSpec((1, dh, dh), lambda h: (h, 0, 0)),
        out_shape=jax.ShapeDtypeStruct((heads, dh, dh), F32),
        cost_estimate=cost(2 * heads * toks * dh * dh, 4 * heads * toks * dh),
        name="block_states",
    )(keys, values)


def local_body(q_ref, k_ref, v_ref, w_ref, out_ref):
    stretches = q_ref.shape[1] // CH
    key_pos = lax.broadcasted_iota(jnp.int32, (CH, CH), 0)
    tok_pos = lax.broadcasted_iota(jnp.int32, (CH, CH), 1)
    dist = jnp.bitwise_xor(key_pos, tok_pos)
    level = jnp.zeros((CH, CH), jnp.int32)
    for bit in range(CH.bit_length() - 1):
        level = level + (dist >= (1 << bit)).astype(jnp.int32)
    level = jnp.where(key_pos <= tok_pos, level, -1)
    first = CH.bit_length()
    states = []
    for c in range(stretches):
        rows = slice(c * CH, (c + 1) * CH)
        q, k, v = q_ref[0, rows, :], k_ref[0, rows, :], v_ref[0, rows, :]
        weights = w_ref[0, :, rows]
        mix = jnp.zeros((CH, CH), F32)
        for lev in range(first):
            mix = jnp.where(level == lev, weights[lev : lev + 1, :], mix)
        probs = (dot11(k, q) * mix).astype(BF16)
        total = dot00(v, probs)
        if c < stretches - 1:
            states.append(dot00(v, k))
        span, step = 1, 0
        while span < stretches:
            if c & span:
                base = (c // (2 * span)) * 2 * span
                left = states[base]
                for other in range(base + 1, base + span):
                    left = left + states[other]
                lev = first + step
                total = total + dot11(left.astype(BF16), q) * weights[lev : lev + 1, :]
            span, step = span * 2, step + 1
        out_ref[0, :, rows] = total


def local_part(queries, keys, values, weights, head):
    _, toks, dh = queries.shape
    levels = weights.shape[1]
    spec = pl.BlockSpec((1, toks, dh), lambda i: (head, 0, 0))
    return pl.pallas_call(
        local_body,
        grid=(1,),
        in_specs=[spec, spec, spec, pl.BlockSpec((1, levels, toks), lambda i: (head, 0, 0))],
        out_specs=pl.BlockSpec((1, dh, toks), lambda i: (0, 0, 0)),
        out_shape=jax.ShapeDtypeStruct((1, dh, toks), F32),
        cost_estimate=cost(2 * 5 * toks * dh * dh, 10 * toks * dh),
        name="local_part",
    )(queries, keys, values, weights)


def far_body(heads, bits, table_ref, *refs):
    half = heads + 2
    sib_refs = refs[2 * half : 2 * half + bits]
    gain_ref = refs[2 * half + bits]
    outs = refs[2 * half + bits + 1 :]
    first = CH.bit_length() + 3
    for side in range(2):
        acc_refs = refs[side * half : side * half + heads]
        q_ref, w_ref = refs[side * half + heads : (side + 1) * half]
        for h in range(heads):
            total = acc_refs[h][0]
            q = q_ref[h]
            for bit in range(bits):
                flag = table_ref[8 + bit].astype(F32)
                row = w_ref[h, first + bit : first + bit + 1, :] * flag
                total = total + dot11(sib_refs[bit][h], q) * row
            mean_sq = jnp.mean(total * total, axis=0, keepdims=True)
            normed = total * lax.rsqrt(mean_sq + 1e-06) * gain_ref[h]
            outs[side][0, :, h * CH : (h + 1) * CH] = normed.astype(BF16).T


def far_part(table, accs, queries, weights, sibs, gains, start, count):
    heads, toks, dh = queries.shape
    levels = weights.shape[1]
    bits = len(sibs)
    in_specs = []
    for side in range(2):
        pick = lambda j, tab, side=side: tab[2 * (start + j) + side]
        in_specs += [pl.BlockSpec((1, dh, CH), lambda j, tab, pick=pick: (0, 0, pick(j, tab)))] * heads
        in_specs.append(pl.BlockSpec((heads, CH, dh), lambda j, tab, pick=pick: (0, pick(j, tab), 0)))
        in_specs.append(pl.BlockSpec((heads, levels, CH), lambda j, tab, pick=pick: (0, 0, pick(j, tab))))
    in_specs += [pl.BlockSpec((heads, dh, dh), lambda j, tab: (0, 0, 0))] * (bits + 1)
    out_spec = pl.BlockSpec((1, CH, heads * dh), lambda j, tab: (j, 0, 0))
    out_shape = jax.ShapeDtypeStruct((count, CH, heads * dh), BF16)
    side_args = [*accs, queries, weights]
    return pl.pallas_call(
        lambda *refs: far_body(heads, bits, *refs),
        grid_spec=pltpu.PrefetchScalarGridSpec(
            num_scalar_prefetch=1,
            grid=(count,),
            in_specs=in_specs,
            out_specs=[out_spec, out_spec],
        ),
        out_shape=[out_shape, out_shape],
        cost_estimate=cost(2 * 2 * count * 4 * heads * CH * dh * dh, 2 * count * heads * CH * dh * 8),
        name="far_part",
    )(table, *side_args, *side_args, *sibs, gains)


def project_body(adds, own_ref, other_ref, wa_ref, wb_ref, *refs):
    total = jnp.dot(own_ref[0], wa_ref[...], preferred_element_type=F32)
    total = total + jnp.dot(other_ref[0], wb_ref[...], preferred_element_type=F32)
    for ref in refs[:adds]:
        total = total + ref[...].astype(F32)
    refs[adds][...] = total.astype(refs[adds].dtype)


def project(own, other, block, w_own, w_other, col_start, cols, adds=(), out_dtype=BF16, tile=512):
    _, rows, depth = own.shape
    first = col_start // tile
    row_spec = pl.BlockSpec((1, rows, depth), lambda n: (block, 0, 0))
    w_spec = pl.BlockSpec((depth, tile), lambda n: (0, first + n))
    tile_spec = pl.BlockSpec((rows, tile), lambda n: (0, n))
    return pl.pallas_call(
        lambda *refs: project_body(len(adds), *refs),
        grid=(cols // tile,),
        in_specs=[row_spec, row_spec, w_spec, w_spec] + [tile_spec] * len(adds),
        out_specs=tile_spec,
        out_shape=jax.ShapeDtypeStruct((rows, cols), out_dtype),
        cost_estimate=cost(2 * rows * cols * depth * 2, 4 * depth * cols + 4 * rows * cols),
        name="project",
    )(own, other, w_own, w_other, *adds)


def on_device(queries, key_rows, value_rows, level_weight, norm_gain, out_weight):
    toks, heads, dh = queries.shape
    q = jnp.transpose(queries, (1, 0, 2))
    k = jnp.transpose(key_rows, (1, 0, 2))
    v = jnp.transpose(value_rows, (1, 0, 2))
    w = jnp.transpose(level_weight, (1, 2, 0))
    width = out_weight.shape[1]
    half = width // 2
    ctx = lax.axis_index("ctx")
    place = lax.axis_index("head")
    z, core = place // 2, place % 2

    def along_z(x, step):
        pairs = [(2 * i + c, 2 * ((i + step) % 4) + c) for i in range(4) for c in range(2)]
        return lax.ppermute(x, "head", pairs)

    def across_cores(x):
        return lax.ppermute(x, "head", [(i, i ^ 1) for i in range(8)])

    def ctx_swap(x, bit):
        swap = ((1, 0, 3, 2), (3, 2, 1, 0))[bit % 2]
        if bit < 2:
            pairs = [(4 * y + i, 4 * y + swap[i]) for y in range(4) for i in range(4)]
        else:
            pairs = [(4 * i + x, 4 * swap[i] + x) for i in range(4) for x in range(4)]
        return lax.ppermute(x, "ctx", pairs)

    gains = jnp.broadcast_to(norm_gain[:, :, None], (heads, dh, CH))
    order = jnp.stack([(z + 2) % 4, (z + 1) % 4, (z + 3) % 4, z]).astype(jnp.int32)
    picks = jnp.stack([2 * order + core, 2 * order + 1 - core], axis=1).reshape(-1)
    flags = (ctx >> jnp.arange(4)) & 1
    table = jnp.concatenate([picks, flags]).astype(jnp.int32)

    running = block_states(k, v)
    w_other = across_cores(out_weight)
    accs = [local_part(q, k, v, w, h) for h in range(heads)]
    sibs = []
    for bit in range(4):
        got = ctx_swap(running.astype(BF16), bit)
        sibs.append(got)
        if bit < 3:
            running = running + got.astype(F32)

    own1, send1 = far_part(table, accs, q, w, sibs, gains, 0, 1)
    other1 = across_cores(send1)
    own2, send2 = far_part(table, accs, q, w, sibs, gains, 1, 3)
    other2 = across_cores(send2)

    relay_up = along_z(project(own1, other1, 0, out_weight, w_other, 0, half), 1)
    relay_down = along_z(project(own1, other1, 0, out_weight, w_other, half, half), -1)
    direct_up = along_z(project(own2, other2, 0, out_weight, w_other, half, half), 1)
    direct_down = along_z(project(own2, other2, 1, out_weight, w_other, 0, half), -1)
    joined_up = along_z(project(own2, other2, 0, out_weight, w_other, 0, half, (relay_up,)), 1)
    joined_down = along_z(project(own2, other2, 1, out_weight, w_other, half, half, (relay_down,)), -1)
    left = project(own2, other2, 2, out_weight, w_other, 0, half, (direct_down,), F32)
    right = project(own2, other2, 2, out_weight, w_other, half, half, (direct_up,), F32)
    left = (left + joined_up.astype(F32)).astype(BF16)
    right = (right + joined_down.astype(F32)).astype(BF16)
    return jnp.concatenate([left, right], axis=1)


def solution(mesh):
    placed = (
        P("ctx", "head", None),
        P("ctx", "head", None),
        P("ctx", "head", None),
        P("ctx", "head", None),
        P("head", None),
        P("head", None),
    )
    return jax.shard_map(
        on_device, mesh=mesh, in_specs=placed, out_specs=P(("ctx", "head"), None), check_vma=False
    )
```

```python
import jax
import jax.numpy as jnp
from jax import lax
from jax.experimental import pallas as pl
from jax.experimental.pallas import tpu as pltpu
from jax.sharding import PartitionSpec as P

CH = 128
F32 = jnp.float32
BF16 = jnp.bfloat16
VMEM = pl.BlockSpec(memory_space=pltpu.VMEM)
LOCAL_LEVELS = CH.bit_length()


def dot00(a, b):
    return lax.dot_general(a, b, (((0,), (0,)), ((), ())), preferred_element_type=F32)


def dot11(a, b):
    return lax.dot_general(a, b, (((1,), (1,)), ((), ())), preferred_element_type=F32)


def cost(flops, byte_count):
    return pl.CostEstimate(flops=flops, bytes_accessed=byte_count, transcendentals=0)


def vmem(megabytes):
    return pltpu.CompilerParams(vmem_limit_bytes=megabytes << 20)


def local_body(heads, q_ref, k_ref, v_ref, w_ref, out_ref):
    stretches = q_ref.shape[1] // CH
    key_pos = lax.broadcasted_iota(jnp.int32, (CH, CH), 0)
    tok_pos = lax.broadcasted_iota(jnp.int32, (CH, CH), 1)
    dist = jnp.bitwise_xor(key_pos, tok_pos)
    level = jnp.zeros((CH, CH), jnp.int32)
    for bit in range(LOCAL_LEVELS - 1):
        level = level + (dist >= (1 << bit)).astype(jnp.int32)
    level = jnp.where(key_pos <= tok_pos, level, -1)
    for slot, h in enumerate(heads):
        states = []
        for c in range(stretches):
            rows = slice(c * CH, (c + 1) * CH)
            q, k, v = q_ref[h, rows, :], k_ref[h, rows, :], v_ref[h, rows, :]
            weights = w_ref[h, :, rows]
            mix = jnp.zeros((CH, CH), F32)
            for lev in range(LOCAL_LEVELS):
                mix = jnp.where(level == lev, weights[lev : lev + 1, :], mix)
            lefts, levs = [], []
            span, step = 1, 0
            while span < stretches:
                if c & span:
                    base = (c // (2 * span)) * 2 * span
                    left = states[base]
                    for other in range(base + 1, base + span):
                        left = left + states[other]
                    lefts.append(left.astype(BF16))
                    levs.append(LOCAL_LEVELS + step)
                span, step = span * 2, step + 1
            read = dot11(jnp.concatenate([k] + lefts, axis=0), q)
            probs = (read[:CH] * mix).astype(BF16)
            if c < stretches - 1:
                both = dot00(v, jnp.concatenate([probs, k], axis=1))
                total = both[:, :CH]
                states.append(both[:, CH:])
            else:
                total = dot00(v, probs)
            for i, lev in enumerate(levs):
                total = total + read[(1 + i) * CH : (2 + i) * CH] * weights[lev : lev + 1, :]
            out_ref[slot, :, rows] = total


def local_part(queries, keys, values, weights, heads):
    _, toks, dh = queries.shape
    count = len(heads)
    return pl.pallas_call(
        lambda *refs: local_body(heads, *refs),
        in_specs=[VMEM] * 4,
        out_specs=VMEM,
        out_shape=jax.ShapeDtypeStruct((count, dh, toks), F32),
        cost_estimate=cost(10 * count * toks * dh * dh, 10 * count * toks * dh),
        compiler_params=vmem(16),
        name="local_part",
    )(queries, keys, values, weights)


def far_body(parts, first, away, steps, q_ref, w_ref, gain_ref, sib_refs, acc_refs, out_ref):
    bits = len(sib_refs)
    ctx, place = lax.axis_index("ctx"), lax.axis_index("head")
    z, side = place // 2, (place + away) % 2
    flags = [((ctx >> bit) & 1).astype(F32) for bit in range(bits)]
    for j, step in enumerate(steps):
        start = pl.multiple_of((2 * ((z + step) % 4) + side) * CH, CH)
        span = pl.ds(start, CH)
        for a, group in enumerate(parts):
            for slot, h in enumerate(group):
                sib = jnp.concatenate([ref[h] for ref in sib_refs], axis=0)
                read = dot11(sib, q_ref[h, span, :])
                total = acc_refs[a][slot, :, span]
                for bit in range(bits):
                    row = w_ref[h, first + bit : first + bit + 1, span] * flags[bit]
                    total = total + read[bit * CH : (bit + 1) * CH] * row
                mean_sq = jnp.mean(total * total, axis=0, keepdims=True)
                normed = total * lax.rsqrt(mean_sq + 1e-06) * gain_ref[h]
                out_ref[j, :, h * CH : (h + 1) * CH] = normed.astype(BF16).T


def far_part(accs, parts, queries, weights, sibs, gains, away, steps):
    heads, toks, dh = queries.shape
    count = len(steps)
    first = LOCAL_LEVELS + (toks // CH).bit_length() - 1
    bits = len(sibs)

    def body(q_ref, w_ref, gain_ref, *refs):
        far_body(parts, first, away, steps, q_ref, w_ref, gain_ref, refs[:bits], refs[bits:-1], refs[-1])

    return pl.pallas_call(
        body,
        in_specs=[VMEM] * (3 + bits + len(accs)),
        out_specs=VMEM,
        out_shape=jax.ShapeDtypeStruct((count, CH, heads * dh), BF16),
        cost_estimate=cost(1000, 1000),
        compiler_params=vmem(16),
        name="far_part",
    )(queries, weights, gains, *sibs, *accs)


def project_body(block, col_start, tile, adds, own_ref, other_ref, wa_ref, wb_ref, *refs):
    out_ref = refs[-1]
    for n in range(out_ref.shape[1] // tile):
        here = slice(n * tile, (n + 1) * tile)
        there = slice(col_start + n * tile, col_start + (n + 1) * tile)
        total = jnp.dot(own_ref[block], wa_ref[:, there], preferred_element_type=F32)
        total = total + jnp.dot(other_ref[block], wb_ref[:, there], preferred_element_type=F32)
        for source, offset in adds:
            if offset <= n * tile < offset + refs[source].shape[1]:
                part = slice(n * tile - offset, (n + 1) * tile - offset)
                total = total + refs[source][:, part].astype(F32)
        out_ref[:, here] = total.astype(out_ref.dtype)


def project(own, other, block, w_own, w_other, col_start, cols, adds=(), out_dtype=BF16, tile=512):
    _, rows, depth = own.shape
    places = [(i, offset) for i, (_, offset) in enumerate(adds)]
    return pl.pallas_call(
        lambda *refs: project_body(block, col_start, tile, places, *refs),
        in_specs=[VMEM] * (4 + len(adds)),
        out_specs=VMEM,
        out_shape=jax.ShapeDtypeStruct((rows, cols), out_dtype),
        cost_estimate=cost(1000, 1000),
        compiler_params=vmem(24),
        name="project",
    )(own, other, w_own, w_other, *[x for x, _ in adds])


def finish_body(own_ref, left_ref, right_ref, out_ref):
    tile = out_ref.shape[1]
    half = left_ref.shape[1]
    step = pl.program_id(0)
    span = pl.ds(pl.multiple_of(step * tile, tile), tile)

    @pl.when(step * tile < half)
    def _():
        out_ref[...] = (own_ref[:, span] + left_ref[:, span].astype(F32)).astype(out_ref.dtype)

    @pl.when(step * tile >= half)
    def _():
        late = pl.ds(pl.multiple_of(step * tile - half, tile), tile)
        out_ref[...] = (own_ref[:, span] + right_ref[:, late].astype(F32)).astype(out_ref.dtype)


def finish(own, left, right, tile=1280):
    rows, cols = own.shape
    return pl.pallas_call(
        finish_body,
        grid=(cols // tile,),
        in_specs=[VMEM] * 3,
        out_specs=pl.BlockSpec((rows, tile), lambda n: (0, n)),
        out_shape=jax.ShapeDtypeStruct((rows, cols), BF16),
        cost_estimate=cost(rows * cols, 10 * rows * cols),
        compiler_params=vmem(16),
        name="finish",
    )(own, left, right)


def on_device(queries, key_rows, value_rows, level_weight, norm_gain, out_weight):
    toks, heads, dh = queries.shape
    q = jnp.transpose(queries, (1, 0, 2))
    k = jnp.transpose(key_rows, (1, 0, 2))
    v = jnp.transpose(value_rows, (1, 0, 2))
    w = jnp.transpose(level_weight, (1, 2, 0))
    width = out_weight.shape[1]
    half = width // 2

    def along_z(x, step):
        pairs = [(2 * i + c, 2 * ((i + step) % 4) + c) for i in range(4) for c in range(2)]
        return lax.ppermute(x, "head", pairs)

    def across_cores(x):
        return lax.ppermute(x, "head", [(i, i ^ 1) for i in range(8)])

    def ctx_swap(x, bit):
        swap = ((1, 0, 3, 2), (3, 2, 1, 0))[bit % 2]
        if bit < 2:
            pairs = [(4 * y + i, 4 * y + swap[i]) for y in range(4) for i in range(4)]
        else:
            pairs = [(4 * i + x, 4 * swap[i] + x) for i in range(4) for x in range(4)]
        return lax.ppermute(x, "ctx", pairs)

    gains = jnp.broadcast_to(norm_gain[:, :, None], (heads, dh, CH))
    message = jnp.einsum("hse,hsd->hed", v, k, preferred_element_type=F32).astype(BF16)
    w_other = across_cores(out_weight)
    parts = [(0,), (1,), (2,), (3, 4)]
    sibs, accs = [], []
    for bit in range(4):
        got = ctx_swap(message, bit)
        tied, _ = lax.optimization_barrier((w, message))
        acc = local_part(q, k, v, tied, parts[bit])
        got, acc = lax.optimization_barrier((got, acc))
        if bit == 2:
            got, w_other = lax.optimization_barrier((got, w_other))
        sibs.append(got)
        accs.append(acc)
        if bit < 3:
            message = (message.astype(F32) + got.astype(F32)).astype(BF16)

    send1 = far_part(accs, parts, q, w, sibs, gains, 1, (2,))
    other1 = across_cores(send1)
    own1 = far_part(accs, parts, q, w, sibs, gains, 0, (2,))
    first_up = project(own1, other1, 0, out_weight, w_other, 0, half)
    first_down = project(own1, other1, 0, out_weight, w_other, half, half)
    late_q, first_up, first_down = lax.optimization_barrier((q, first_up, first_down))
    relay_up = along_z(first_up, 1)
    relay_down = along_z(first_down, -1)
    send2 = far_part(accs, parts, late_q, w, sibs, gains, 1, (1, 3, 0))
    other2 = across_cores(send2)
    own2 = far_part(accs, parts, late_q, w, sibs, gains, 0, (1, 3, 0))
    direct_up = along_z(project(own2, other2, 0, out_weight, w_other, half, half), 1)
    direct_down = along_z(project(own2, other2, 1, out_weight, w_other, 0, half), -1)
    joined_up = along_z(project(own2, other2, 0, out_weight, w_other, 0, half, ((relay_up, 0),)), 1)
    joined_down = along_z(project(own2, other2, 1, out_weight, w_other, half, half, ((relay_down, 0),)), -1)
    mine = project(
        own2, other2, 2, out_weight, w_other, 0, width, ((direct_down, 0), (direct_up, half)), F32
    )
    return finish(mine, joined_up, joined_down)


def solution(mesh):
    placed = (
        P("ctx", "head", None),
        P("ctx", "head", None),
        P("ctx", "head", None),
        P("ctx", "head", None),
        P("head", None),
        P("head", None),
    )
    return jax.shard_map(
        on_device, mesh=mesh, in_specs=placed, out_specs=P(("ctx", "head"), None), check_vma=False
    )
```

```python
import jax
import jax.numpy as jnp
from jax import lax
from jax.experimental import pallas as pl
from jax.experimental.pallas import tpu as pltpu
from jax.sharding import PartitionSpec as P

CH = 128
F32 = jnp.float32
BF16 = jnp.bfloat16
VMEM = pl.BlockSpec(memory_space=pltpu.VMEM)
LOCAL_LEVELS = CH.bit_length()
FINISH_TILE = 1280
MINE_FLOPS = 1000
FAR_FLOPS = 1000


def dot00(a, b):
    return lax.dot_general(a, b, (((0,), (0,)), ((), ())), preferred_element_type=F32)


def dot11(a, b):
    return lax.dot_general(a, b, (((1,), (1,)), ((), ())), preferred_element_type=F32)


def cost(flops, byte_count):
    return pl.CostEstimate(flops=flops, bytes_accessed=byte_count, transcendentals=0)


def vmem(megabytes):
    return pltpu.CompilerParams(vmem_limit_bytes=megabytes << 20)


def local_body(heads, q_ref, k_ref, v_ref, w_ref, out_ref):
    stretches = q_ref.shape[1] // CH
    key_pos = lax.broadcasted_iota(jnp.int32, (CH, CH), 0)
    tok_pos = lax.broadcasted_iota(jnp.int32, (CH, CH), 1)
    dist = jnp.bitwise_xor(key_pos, tok_pos)
    level = jnp.zeros((CH, CH), jnp.int32)
    for bit in range(LOCAL_LEVELS - 1):
        level = level + (dist >= (1 << bit)).astype(jnp.int32)
    level = jnp.where(key_pos <= tok_pos, level, -1)
    for slot, h in enumerate(heads):
        states = []
        for c in range(stretches):
            rows = slice(c * CH, (c + 1) * CH)
            q, k, v = q_ref[h, rows, :], k_ref[h, rows, :], v_ref[h, rows, :]
            weights = w_ref[h, :, rows]
            mix = jnp.zeros((CH, CH), F32)
            for lev in range(LOCAL_LEVELS):
                mix = jnp.where(level == lev, weights[lev : lev + 1, :], mix)
            lefts, levs = [], []
            span, step = 1, 0
            while span < stretches:
                if c & span:
                    base = (c // (2 * span)) * 2 * span
                    left = states[base]
                    for other in range(base + 1, base + span):
                        left = left + states[other]
                    lefts.append(left.astype(BF16))
                    levs.append(LOCAL_LEVELS + step)
                span, step = span * 2, step + 1
            read = dot11(jnp.concatenate([k] + lefts, axis=0), q)
            probs = (read[:CH] * mix).astype(BF16)
            if c < stretches - 1:
                both = dot00(v, jnp.concatenate([probs, k], axis=1))
                total = both[:, :CH]
                states.append(both[:, CH:])
            else:
                total = dot00(v, probs)
            for i, lev in enumerate(levs):
                total = total + read[(1 + i) * CH : (2 + i) * CH] * weights[lev : lev + 1, :]
            out_ref[slot, :, rows] = total


def local_part(queries, keys, values, weights, heads, held=()):
    _, toks, dh = queries.shape
    count = len(heads)
    return pl.pallas_call(
        lambda *refs: local_body(heads, *refs[:4], refs[-1]),
        in_specs=[VMEM] * (4 + len(held)),
        out_specs=VMEM,
        out_shape=jax.ShapeDtypeStruct((count, dh, toks), F32),
        cost_estimate=cost(10 * count * toks * dh * dh, 10 * count * toks * dh),
        compiler_params=vmem(16),
        name="local_part",
    )(queries, keys, values, weights, *held)


def far_body(parts, first, away, steps, q_ref, w_ref, gain_ref, sib_refs, acc_refs, out_ref):
    ctx, place = lax.axis_index("ctx"), lax.axis_index("head")
    z, side = place // 2, (place + away) % 2
    bits = [((ctx >> bit) & 1).astype(F32) for bit in range(4)]
    for j, step in enumerate(steps):
        start = pl.multiple_of((2 * ((z + step) % 4) + side) * CH, CH)
        span = pl.ds(start, CH)
        for a, group in enumerate(parts):
            for slot, h in enumerate(group):
                sib = jnp.concatenate([ref[h] for ref in sib_refs], axis=0)
                read = dot11(sib, q_ref[h, span, :])
                total = acc_refs[a][slot, :, span]
                for bit, scale in enumerate(bits):
                    row = w_ref[h, first + bit : first + bit + 1, span] * scale
                    total = total + read[bit * CH : (bit + 1) * CH] * row
                mean_sq = jnp.mean(total * total, axis=0, keepdims=True)
                normed = total * lax.rsqrt(mean_sq + 1e-06) * gain_ref[h]
                out_ref[j, :, h * CH : (h + 1) * CH] = normed.astype(BF16).T


def far_part(accs, parts, queries, weights, sibs, gains, away, steps, flops=1000):
    heads, toks, dh = queries.shape
    count = len(steps)
    first = LOCAL_LEVELS + (toks // CH).bit_length() - 1
    held = len(sibs)

    def body(q_ref, w_ref, gain_ref, *refs):
        far_body(parts, first, away, steps, q_ref, w_ref, gain_ref, refs[:held], refs[held:-1], refs[-1])

    return pl.pallas_call(
        body,
        in_specs=[VMEM] * (3 + held + len(accs)),
        out_specs=VMEM,
        out_shape=jax.ShapeDtypeStruct((count, CH, heads * dh), BF16),
        cost_estimate=cost(flops, 1000),
        compiler_params=vmem(16),
        name="far_part",
    )(queries, weights, gains, *sibs, *accs)


def tiles_of(cols, tile=512):
    return [(n, min(tile, cols - n)) for n in range(0, cols, tile)]


def project_body(pairs, col_start, adds, refs):
    out_ref = refs[-1]
    sources = refs[2 * len(pairs) : -1]
    cuts = sorted({0, out_ref.shape[1], *adds})
    places = [(lo + n, size) for lo, hi in zip(cuts, cuts[1:]) for n, size in tiles_of(hi - lo)]
    for n, size in places:
        there = slice(col_start + n, col_start + n + size)
        total = None
        for i, block in enumerate(pairs):
            part = jnp.dot(refs[2 * i][block], refs[2 * i + 1][:, there], preferred_element_type=F32)
            total = part if total is None else total + part
        for source, lo in zip(sources, adds):
            if lo <= n < lo + source.shape[1]:
                total = total + source[:, n - lo : n - lo + size].astype(F32)
        out_ref[:, n : n + size] = total.astype(out_ref.dtype)


def project(pairs, col_start, cols, adds=(), out_dtype=BF16, flops=1000):
    rows = pairs[0][0].shape[1]
    blocks = [block for _, block, _ in pairs]
    args = [x for value, _, weight in pairs for x in (value, weight)]
    return pl.pallas_call(
        lambda *refs: project_body(blocks, col_start, [lo for _, lo in adds], refs),
        in_specs=[VMEM] * (len(args) + len(adds)),
        out_specs=VMEM,
        out_shape=jax.ShapeDtypeStruct((rows, cols), out_dtype),
        cost_estimate=cost(flops, 1000),
        compiler_params=vmem(24),
        name="project",
    )(*args, *[x for x, _ in adds])


def finish_body(own_ref, right_ref, left_ref, out_ref, hold_ref, sems):
    split = left_ref.shape[1]
    copies = []
    for late_ref, start in ((left_ref, 0), (right_ref, split)):
        for n, size in tiles_of(late_ref.shape[1], FINISH_TILE):
            there = slice(start + n, start + n + size)
            total = own_ref[:, there] + late_ref[:, n : n + size].astype(F32)
            hold_ref[:, there] = total.astype(BF16)
            i = len(copies)
            copies.append(pltpu.make_async_copy(hold_ref.at[:, there], out_ref.at[:, there], sems.at[i]))
            copies[-1].start()
    for copy in copies:
        copy.wait()


def finish(own, left, right):
    rows, width = own.shape
    count = len(tiles_of(left.shape[1], FINISH_TILE)) + len(tiles_of(right.shape[1], FINISH_TILE))
    return pl.pallas_call(
        finish_body,
        in_specs=[VMEM] * 3,
        out_specs=pl.BlockSpec(memory_space=pl.ANY),
        out_shape=jax.ShapeDtypeStruct((rows, width), BF16),
        scratch_shapes=[pltpu.VMEM((rows, width), BF16), pltpu.SemaphoreType.DMA((count,))],
        cost_estimate=cost(1000, 1000),
        compiler_params=vmem(16),
        name="finish",
    )(own, right, left)


def on_device(queries, key_rows, value_rows, level_weight, norm_gain, out_weight):
    toks, heads, dh = queries.shape
    q = jnp.transpose(queries, (1, 0, 2))
    k = jnp.transpose(key_rows, (1, 0, 2))
    v = jnp.transpose(value_rows, (1, 0, 2))
    w = jnp.transpose(level_weight, (1, 2, 0))
    width = out_weight.shape[1]
    split = width // 2
    rest = width - split

    def along_z(x, step):
        pairs = [(2 * i + c, 2 * ((i + step) % 4) + c) for i in range(4) for c in range(2)]
        return lax.ppermute(x, "head", pairs)

    def across_cores(x):
        return lax.ppermute(x, "head", [(i, i ^ 1) for i in range(8)])

    def ctx_swap(x, bit):
        swap = ((1, 0, 3, 2), (3, 2, 1, 0))[bit % 2]
        if bit < 2:
            pairs = [(4 * y + i, 4 * y + swap[i]) for y in range(4) for i in range(4)]
        else:
            pairs = [(4 * i + x, 4 * swap[i] + x) for i in range(4) for x in range(4)]
        return lax.ppermute(x, "ctx", pairs)

    gains = jnp.broadcast_to(norm_gain[:, :, None], (heads, dh, CH))
    message = jnp.einsum("hse,hsd->hed", v, k, preferred_element_type=F32).astype(BF16)
    w_other = across_cores(out_weight)
    parts = [(0,), (1,), (2,), (3, 4)]
    sibs, accs = [], []
    for bit in range(4):
        got = ctx_swap(message, bit)
        tied, _ = lax.optimization_barrier((w, message))
        held = (out_weight,) if bit == 2 else ()
        got, acc = lax.optimization_barrier((got, local_part(q, k, v, tied, parts[bit], held)))
        if bit == 2:
            got, w_other = lax.optimization_barrier((got, w_other))
        sibs.append(got)
        accs.append(acc)
        if bit < 3:
            message = (message.astype(F32) + got.astype(F32)).astype(BF16)

    send1 = far_part(accs, parts, q, w, sibs, gains, 1, (2,))
    other1 = across_cores(send1)
    own1 = far_part(accs, parts, q, w, sibs, gains, 0, (2,))
    early_up = project([(own1, 0, out_weight)], 0, split, (), F32)
    early_down = project([(own1, 0, out_weight)], split, rest, (), F32)
    first_up = project([(other1, 0, w_other)], 0, split, ((early_up, 0),))
    late_other, first_up = lax.optimization_barrier((other1, first_up))
    first_down = project([(late_other, 0, w_other)], split, rest, ((early_down, 0),))
    late_q, first_down = lax.optimization_barrier((q, first_down))
    relay_up = along_z(first_up, 1)
    relay_down = along_z(first_down, -1)
    send2 = far_part(accs, parts, late_q, w, sibs, gains, 1, (1, 3, 0))
    other2 = across_cores(send2)
    own2 = far_part(accs, parts, late_q, w, sibs, gains, 0, (1, 3, 0), FAR_FLOPS)

    def block(i):
        return [(own2, i, out_weight), (other2, i, w_other)]

    next_up = project(block(0), split, rest)
    next_down = project(block(1), 0, split)
    direct_up = along_z(next_up, 1)
    direct_down = along_z(next_down, -1)
    joined_up = along_z(project(block(0), 0, split, ((relay_up, 0),)), 1)
    joined_down = along_z(project(block(1), split, rest, ((relay_down, 0),)), -1)
    mine = project(block(2), 0, width, ((direct_down, 0), (direct_up, split)), F32, MINE_FLOPS)
    return finish(mine, joined_up, joined_down)


def solution(mesh):
    placed = (
        P("ctx", "head", None),
        P("ctx", "head", None),
        P("ctx", "head", None),
        P("ctx", "head", None),
        P("head", None),
        P("head", None),
    )
    return jax.shard_map(
        on_device, mesh=mesh, in_specs=placed, out_specs=P(("ctx", "head"), None), check_vma=False
    )
```

```python
import jax
import jax.numpy as jnp
from jax import lax
from jax.experimental import pallas as pl
from jax.experimental.pallas import tpu as pltpu
from jax.sharding import PartitionSpec as P

CH = 128
F32 = jnp.float32
BF16 = jnp.bfloat16
VMEM = pl.BlockSpec(memory_space=pltpu.VMEM)
LOCAL_LEVELS = CH.bit_length()
FINISH_TILE = 1280
MINE_FLOPS = 1000
FAR_FLOPS = 1000


def dot00(a, b):
    return lax.dot_general(a, b, (((0,), (0,)), ((), ())), preferred_element_type=F32)


def dot11(a, b):
    return lax.dot_general(a, b, (((1,), (1,)), ((), ())), preferred_element_type=F32)


def cost(flops, byte_count):
    return pl.CostEstimate(flops=flops, bytes_accessed=byte_count, transcendentals=0)


def vmem(megabytes):
    return pltpu.CompilerParams(vmem_limit_bytes=megabytes << 20)


def local_body(heads, q_ref, k_ref, v_ref, w_ref, out_ref):
    stretches = q_ref.shape[1] // CH
    key_pos = lax.broadcasted_iota(jnp.int32, (CH, CH), 0)
    tok_pos = lax.broadcasted_iota(jnp.int32, (CH, CH), 1)
    dist = jnp.bitwise_xor(key_pos, tok_pos)
    level = jnp.zeros((CH, CH), jnp.int32)
    for bit in range(LOCAL_LEVELS - 1):
        level = level + (dist >= (1 << bit)).astype(jnp.int32)
    level = jnp.where(key_pos <= tok_pos, level, -1)
    for slot, h in enumerate(heads):
        states = []
        for c in range(stretches):
            rows = slice(c * CH, (c + 1) * CH)
            q, k, v = q_ref[h, rows, :], k_ref[h, rows, :], v_ref[h, rows, :]
            weights = w_ref[h, :, rows]
            mix = jnp.zeros((CH, CH), F32)
            for lev in range(LOCAL_LEVELS):
                mix = jnp.where(level == lev, weights[lev : lev + 1, :], mix)
            lefts, levs = [], []
            span, step = 1, 0
            while span < stretches:
                if c & span:
                    base = (c // (2 * span)) * 2 * span
                    left = states[base]
                    for other in range(base + 1, base + span):
                        left = left + states[other]
                    lefts.append(left.astype(BF16))
                    levs.append(LOCAL_LEVELS + step)
                span, step = span * 2, step + 1
            read = dot11(jnp.concatenate([k] + lefts, axis=0), q)
            probs = (read[:CH] * mix).astype(BF16)
            if c < stretches - 1:
                both = dot00(v, jnp.concatenate([probs, k], axis=1))
                total = both[:, :CH]
                states.append(both[:, CH:])
            else:
                total = dot00(v, probs)
            for i, lev in enumerate(levs):
                total = total + read[(1 + i) * CH : (2 + i) * CH] * weights[lev : lev + 1, :]
            out_ref[slot, :, rows] = total


def local_part(queries, keys, values, weights, heads, held=()):
    _, toks, dh = queries.shape
    count = len(heads)
    return pl.pallas_call(
        lambda *refs: local_body(heads, *refs[:4], refs[-1]),
        in_specs=[VMEM] * (4 + len(held)),
        out_specs=VMEM,
        out_shape=jax.ShapeDtypeStruct((count, dh, toks), F32),
        cost_estimate=cost(10 * count * toks * dh * dh, 10 * count * toks * dh),
        compiler_params=vmem(16),
        name="local_part",
    )(queries, keys, values, weights, *held)


def far_body(parts, first, away, steps, q_ref, w_ref, gain_ref, sib_refs, acc_refs, out_ref):
    ctx, place = lax.axis_index("ctx"), lax.axis_index("head")
    z, side = place // 2, (place + away) % 2
    bits = [((ctx >> bit) & 1).astype(F32) for bit in range(4)]
    for j, step in enumerate(steps):
        start = pl.multiple_of((2 * ((z + step) % 4) + side) * CH, CH)
        span = pl.ds(start, CH)
        for a, group in enumerate(parts):
            for slot, h in enumerate(group):
                sib = jnp.concatenate([ref[h] for ref in sib_refs], axis=0)
                read = dot11(sib, q_ref[h, span, :])
                total = acc_refs[a][slot, :, span]
                for bit, scale in enumerate(bits):
                    row = w_ref[h, first + bit : first + bit + 1, span] * scale
                    total = total + read[bit * CH : (bit + 1) * CH] * row
                mean_sq = jnp.mean(total * total, axis=0, keepdims=True)
                normed = total * lax.rsqrt(mean_sq + 1e-06) * gain_ref[h]
                out_ref[j, :, h * CH : (h + 1) * CH] = normed.astype(BF16).T


def far_part(accs, parts, queries, weights, sibs, gains, away, steps, flops=1000):
    heads, toks, dh = queries.shape
    count = len(steps)
    first = LOCAL_LEVELS + (toks // CH).bit_length() - 1
    held = len(sibs)

    def body(q_ref, w_ref, gain_ref, *refs):
        far_body(parts, first, away, steps, q_ref, w_ref, gain_ref, refs[:held], refs[held:-1], refs[-1])

    return pl.pallas_call(
        body,
        in_specs=[VMEM] * (3 + held + len(accs)),
        out_specs=VMEM,
        out_shape=jax.ShapeDtypeStruct((count, CH, heads * dh), BF16),
        cost_estimate=cost(flops, 1000),
        compiler_params=vmem(16),
        name="far_part",
    )(queries, weights, gains, *sibs, *accs)


def tiles_of(cols, tile=512):
    return [(n, min(tile, cols - n)) for n in range(0, cols, tile)]


def project_body(blocks, col_start, adds, outs, refs):
    out_refs = refs[len(refs) - len(outs) :]
    sources = refs[2 * len(blocks) : len(refs) - len(outs)]
    spans = [(lo, lo + source.shape[1]) for source, lo in zip(sources, adds)]
    ends = [(sum(outs[:i]), sum(outs[: i + 1])) for i in range(len(outs))]
    cuts = sorted({cut for span in spans + ends for cut in span})
    for n, size in [(lo + n, size) for lo, hi in zip(cuts, cuts[1:]) for n, size in tiles_of(hi - lo)]:
        there = slice(col_start + n, col_start + n + size)
        total = None
        for i, block in enumerate(blocks):
            part = jnp.dot(refs[2 * i][block], refs[2 * i + 1][:, there], preferred_element_type=F32)
            total = part if total is None else total + part
        for source, (lo, hi) in zip(sources, spans):
            if lo <= n < hi:
                total = total + source[:, n - lo : n - lo + size].astype(F32)
        for out_ref, (lo, hi) in zip(out_refs, ends):
            if lo <= n < hi:
                out_ref[:, n - lo : n - lo + size] = total.astype(out_ref.dtype)


def project(pairs, col_start, outs, adds=(), out_dtype=BF16, flops=1000):
    rows = pairs[0][0].shape[1]
    blocks = [block for _, block, _ in pairs]
    args = [x for value, _, weight in pairs for x in (value, weight)]
    shapes = [jax.ShapeDtypeStruct((rows, cols), out_dtype) for cols in outs]
    return pl.pallas_call(
        lambda *refs: project_body(blocks, col_start, [lo for _, lo in adds], outs, refs),
        in_specs=[VMEM] * (len(args) + len(adds)),
        out_specs=[VMEM] * len(outs),
        out_shape=shapes,
        cost_estimate=cost(flops, 1000),
        compiler_params=vmem(24),
        name="project",
    )(*args, *[x for x, _ in adds])


def finish_body(own_ref, left_ref, right_ref, out_ref, hold_ref, sems):
    width = own_ref.shape[1]
    ends, start = left_ref.shape[1], width - right_ref.shape[1]
    cuts = [0, start, ends, width] if start < ends else [0, ends, width]
    copies = []
    for lo, hi in zip(cuts, cuts[1:]):
        for n, size in tiles_of(hi - lo, FINISH_TILE):
            there = slice(lo + n, lo + n + size)
            total = own_ref[:, there]
            if lo < ends:
                total = total + left_ref[:, there].astype(F32)
            if lo >= start:
                total = total + right_ref[:, lo + n - start : lo + n - start + size].astype(F32)
            hold_ref[:, there] = total.astype(BF16)
            i = len(copies)
            copies.append(pltpu.make_async_copy(hold_ref.at[:, there], out_ref.at[:, there], sems.at[i]))
            copies[-1].start()
    for copy in copies:
        copy.wait()


def finish(own, left, right):
    rows, width = own.shape
    count = 3 * len(tiles_of(width, FINISH_TILE))
    return pl.pallas_call(
        finish_body,
        in_specs=[VMEM] * 3,
        out_specs=pl.BlockSpec(memory_space=pl.ANY),
        out_shape=jax.ShapeDtypeStruct((rows, width), BF16),
        scratch_shapes=[pltpu.VMEM((rows, width), BF16), pltpu.SemaphoreType.DMA((count,))],
        cost_estimate=cost(1000, 1000),
        compiler_params=vmem(16),
        name="finish",
    )(own, left, right)


def on_device(queries, key_rows, value_rows, level_weight, norm_gain, out_weight):
    toks, heads, dh = queries.shape
    q = jnp.transpose(queries, (1, 0, 2))
    k = jnp.transpose(key_rows, (1, 0, 2))
    v = jnp.transpose(value_rows, (1, 0, 2))
    w = jnp.transpose(level_weight, (1, 2, 0))
    width = out_weight.shape[1]
    split = width // 2
    rest = width - split

    def along_z(x, step):
        pairs = [(2 * i + c, 2 * ((i + step) % 4) + c) for i in range(4) for c in range(2)]
        return lax.ppermute(x, "head", pairs)

    def across_cores(x):
        return lax.ppermute(x, "head", [(i, i ^ 1) for i in range(8)])

    def swaps(x, along):
        got = []
        for swap in ((3, 2, 1, 0), (1, 0, 3, 2), (2, 3, 0, 1)):
            if along == "x":
                pairs = [(4 * y + i, 4 * y + swap[i]) for y in range(4) for i in range(4)]
            else:
                pairs = [(4 * i + c, 4 * swap[i] + c) for i in range(4) for c in range(4)]
            got.append(lax.ppermute(x, "ctx", pairs))
        return got

    gains = jnp.broadcast_to(norm_gain[:, :, None], (heads, dh, CH))
    message = jnp.einsum("hse,hsd->hed", v, k, preferred_element_type=F32).astype(BF16)
    w_other = across_cores(out_weight)
    parts = [(0, 1, 2), (3, 4)]
    sibs, accs = [], []
    for step, along in enumerate("xy"):
        got = swaps(message, along)
        tied, _ = lax.optimization_barrier((w, message))
        acc = local_part(q, k, v, tied, parts[step], (out_weight,) if step else ())
        low, near, far, acc = lax.optimization_barrier((*got, acc))
        far, low = far.astype(F32), low.astype(F32)
        sibs += [near, (far + low).astype(BF16)]
        accs.append(acc)
        if not step:
            near, w_other = lax.optimization_barrier((near, w_other))
            message = (message.astype(F32) + near.astype(F32) + (far + low)).astype(BF16)

    send1 = far_part(accs, parts, q, w, sibs, gains, 1, (2,))
    other1 = across_cores(send1)
    own1 = far_part(accs, parts, q, w, sibs, gains, 0, (2,))
    (early,) = project([(own1, 0, out_weight)], 0, (width,), (), F32)
    first_up, first_down = project([(other1, 0, w_other)], 0, (split, rest), ((early, 0),))
    late_q, first_up, first_down = lax.optimization_barrier((q, first_up, first_down))
    relay_up = along_z(first_up, 1)
    relay_down = along_z(first_down, -1)
    send2 = far_part(accs, parts, late_q, w, sibs, gains, 1, (1, 3, 0))
    other2 = across_cores(send2)
    own2 = far_part(accs, parts, late_q, w, sibs, gains, 0, (1, 3, 0), FAR_FLOPS)

    def block(i):
        return [(own2, i, out_weight), (other2, i, w_other)]

    direct_up = along_z(project(block(0), split, (rest,))[0], 1)
    direct_down = along_z(project(block(1), 0, (rest,))[0], -1)
    joined_up = along_z(project(block(0), 0, (split,), ((relay_up, 0),))[0], 1)
    joined_down = along_z(project(block(1), rest, (split,), ((relay_down, split - rest),))[0], -1)
    (mine,) = project(block(2), 0, (width,), ((direct_down, 0), (direct_up, split)), F32, MINE_FLOPS)
    return finish(mine, joined_up, joined_down)


def solution(mesh):
    placed = (
        P("ctx", "head", None),
        P("ctx", "head", None),
        P("ctx", "head", None),
        P("ctx", "head", None),
        P("head", None),
        P("head", None),
    )
    return jax.shard_map(
        on_device, mesh=mesh, in_specs=placed, out_specs=P(("ctx", "head"), None), check_vma=False
    )
```

```python
import jax
import jax.numpy as jnp
from jax import lax
from jax.experimental import pallas as pl
from jax.experimental.pallas import tpu as pltpu
from jax.sharding import PartitionSpec as P

CH = 128
F32 = jnp.float32
BF16 = jnp.bfloat16
VMEM = pl.BlockSpec(memory_space=pltpu.VMEM)
LOCAL_LEVELS = CH.bit_length()
FINISH_TILE = 1280
MINE_FLOPS = 1000
FAR_FLOPS = 1000


def dot00(a, b):
    return lax.dot_general(a, b, (((0,), (0,)), ((), ())), preferred_element_type=F32)


def dot11(a, b):
    return lax.dot_general(a, b, (((1,), (1,)), ((), ())), preferred_element_type=F32)


def cost(flops, byte_count):
    return pl.CostEstimate(flops=flops, bytes_accessed=byte_count, transcendentals=0)


def vmem(megabytes):
    return pltpu.CompilerParams(vmem_limit_bytes=megabytes << 20)


def local_body(heads, q_ref, k_ref, v_ref, w_ref, out_ref):
    stretches = q_ref.shape[1] // CH
    key_pos = lax.broadcasted_iota(jnp.int32, (CH, CH), 0)
    tok_pos = lax.broadcasted_iota(jnp.int32, (CH, CH), 1)
    dist = jnp.bitwise_xor(key_pos, tok_pos)
    level = jnp.zeros((CH, CH), jnp.int32)
    for bit in range(LOCAL_LEVELS - 1):
        level = level + (dist >= (1 << bit)).astype(jnp.int32)
    level = jnp.where(key_pos <= tok_pos, level, -1)
    for slot, h in enumerate(heads):
        states = []
        for c in range(stretches):
            rows = slice(c * CH, (c + 1) * CH)
            q, k, v = q_ref[h, rows, :], k_ref[h, rows, :], v_ref[h, rows, :]
            weights = w_ref[h, :, rows]
            mix = jnp.zeros((CH, CH), F32)
            for lev in range(LOCAL_LEVELS):
                mix = jnp.where(level == lev, weights[lev : lev + 1, :], mix)
            lefts, levs = [], []
            span, step = 1, 0
            while span < stretches:
                if c & span:
                    base = (c // (2 * span)) * 2 * span
                    left = states[base]
                    for other in range(base + 1, base + span):
                        left = left + states[other]
                    lefts.append(left.astype(BF16))
                    levs.append(LOCAL_LEVELS + step)
                span, step = span * 2, step + 1
            read = dot11(jnp.concatenate([k] + lefts, axis=0), q)
            probs = (read[:CH] * mix).astype(BF16)
            if c < stretches - 1:
                both = dot00(v, jnp.concatenate([probs, k], axis=1))
                total = both[:, :CH]
                states.append(both[:, CH:])
            else:
                total = dot00(v, probs)
            for i, lev in enumerate(levs):
                total = total + read[(1 + i) * CH : (2 + i) * CH] * weights[lev : lev + 1, :]
            out_ref[slot, :, rows] = total


def local_part(queries, keys, values, weights, heads, held=()):
    _, toks, dh = queries.shape
    count = len(heads)
    return pl.pallas_call(
        lambda *refs: local_body(heads, *refs[:4], refs[-1]),
        in_specs=[VMEM] * (4 + len(held)),
        out_specs=VMEM,
        out_shape=jax.ShapeDtypeStruct((count, dh, toks), F32),
        cost_estimate=cost(10 * count * toks * dh * dh, 10 * count * toks * dh),
        compiler_params=vmem(16),
        name="local_part",
    )(queries, keys, values, weights, *held)


def far_body(parts, first, away, steps, q_ref, w_ref, gain_ref, sib_refs, acc_refs, out_ref):
    ctx, place = lax.axis_index("ctx"), lax.axis_index("head")
    z, side = place // 2, (place + away) % 2
    bits = [((ctx >> bit) & 1).astype(F32) for bit in range(4)]
    for j, step in enumerate(steps):
        start = pl.multiple_of((2 * ((z + step) % 4) + side) * CH, CH)
        span = pl.ds(start, CH)
        for a, group in enumerate(parts):
            for slot, h in enumerate(group):
                sib = jnp.concatenate([ref[h] for ref in sib_refs], axis=0)
                read = dot11(sib, q_ref[h, span, :])
                total = acc_refs[a][slot, :, span]
                for bit, scale in enumerate(bits):
                    row = w_ref[h, first + bit : first + bit + 1, span] * scale
                    total = total + read[bit * CH : (bit + 1) * CH] * row
                mean_sq = jnp.mean(total * total, axis=0, keepdims=True)
                normed = total * lax.rsqrt(mean_sq + 1e-06) * gain_ref[h]
                out_ref[j, :, h * CH : (h + 1) * CH] = normed.astype(BF16).T


def far_part(accs, parts, queries, weights, sibs, gains, away, steps, flops=1000):
    heads, toks, dh = queries.shape
    count = len(steps)
    first = LOCAL_LEVELS + (toks // CH).bit_length() - 1
    held = len(sibs)

    def body(q_ref, w_ref, gain_ref, *refs):
        far_body(parts, first, away, steps, q_ref, w_ref, gain_ref, refs[:held], refs[held:-1], refs[-1])

    return pl.pallas_call(
        body,
        in_specs=[VMEM] * (3 + held + len(accs)),
        out_specs=VMEM,
        out_shape=jax.ShapeDtypeStruct((count, CH, heads * dh), BF16),
        cost_estimate=cost(flops, 1000),
        compiler_params=vmem(16),
        name="far_part",
    )(queries, weights, gains, *sibs, *accs)


def tiles_of(cols, tile=512):
    return [(n, min(tile, cols - n)) for n in range(0, cols, tile)]


def project_body(blocks, col_start, adds, outs, refs):
    out_refs = refs[len(refs) - len(outs) :]
    sources = refs[2 * len(blocks) : len(refs) - len(outs)]
    spans = [(lo, lo + source.shape[1]) for source, lo in zip(sources, adds)]
    ends = [(sum(outs[:i]), sum(outs[: i + 1])) for i in range(len(outs))]
    cuts = sorted({cut for span in spans + ends for cut in span})
    for n, size in [(lo + n, size) for lo, hi in zip(cuts, cuts[1:]) for n, size in tiles_of(hi - lo)]:
        there = slice(col_start + n, col_start + n + size)
        total = None
        for i, block in enumerate(blocks):
            part = jnp.dot(refs[2 * i][block], refs[2 * i + 1][:, there], preferred_element_type=F32)
            total = part if total is None else total + part
        for source, (lo, hi) in zip(sources, spans):
            if lo <= n < hi:
                total = total + source[:, n - lo : n - lo + size].astype(F32)
        for out_ref, (lo, hi) in zip(out_refs, ends):
            if lo <= n < hi:
                out_ref[:, n - lo : n - lo + size] = total.astype(out_ref.dtype)


def project(pairs, col_start, outs, adds=(), out_dtype=BF16, flops=1000):
    rows = pairs[0][0].shape[1]
    blocks = [block for _, block, _ in pairs]
    args = [x for value, _, weight in pairs for x in (value, weight)]
    shapes = [jax.ShapeDtypeStruct((rows, cols), out_dtype) for cols in outs]
    return pl.pallas_call(
        lambda *refs: project_body(blocks, col_start, [lo for _, lo in adds], outs, refs),
        in_specs=[VMEM] * (len(args) + len(adds)),
        out_specs=[VMEM] * len(outs),
        out_shape=shapes,
        cost_estimate=cost(flops, 1000),
        compiler_params=vmem(24),
        name="project",
    )(*args, *[x for x, _ in adds])


def finish_body(starts, own_ref, *refs):
    out_ref, hold_ref, sems = refs[-3:]
    copies = []
    for late_ref, start in zip(refs, starts):
        for n, size in tiles_of(late_ref.shape[1], FINISH_TILE):
            there = slice(start + n, start + n + size)
            total = own_ref[:, there] + late_ref[:, n : n + size].astype(F32)
            hold_ref[:, there] = total.astype(BF16)
            i = len(copies)
            copies.append(pltpu.make_async_copy(hold_ref.at[:, there], out_ref.at[:, there], sems.at[i]))
            copies[-1].start()
    for copy in copies:
        copy.wait()


def finish(own, pieces, so_far=None):
    rows, width = own.shape
    starts = [start for _, start in pieces]
    anywhere = pl.BlockSpec(memory_space=pl.ANY)
    kept = [] if so_far is None else [so_far]
    count = sum(len(tiles_of(piece.shape[1], FINISH_TILE)) for piece, _ in pieces)
    return pl.pallas_call(
        lambda *refs: finish_body(starts, *refs),
        in_specs=[VMEM] * (1 + len(pieces)) + [anywhere] * len(kept),
        out_specs=anywhere,
        out_shape=jax.ShapeDtypeStruct((rows, width), BF16),
        scratch_shapes=[pltpu.VMEM((rows, width), BF16), pltpu.SemaphoreType.DMA((count,))],
        input_output_aliases={1 + len(pieces): 0} if kept else {},
        cost_estimate=cost(1000, 1000),
        compiler_params=vmem(16),
        name="finish",
    )(own, *[piece for piece, _ in pieces], *kept)


def on_device(queries, key_rows, value_rows, level_weight, norm_gain, out_weight):
    toks, heads, dh = queries.shape
    q = jnp.transpose(queries, (1, 0, 2))
    k = jnp.transpose(key_rows, (1, 0, 2))
    v = jnp.transpose(value_rows, (1, 0, 2))
    w = jnp.transpose(level_weight, (1, 2, 0))
    width = out_weight.shape[1]
    split = width // 2
    rest = width - split

    def along_z(x, step):
        pairs = [(2 * i + c, 2 * ((i + step) % 4) + c) for i in range(4) for c in range(2)]
        return lax.ppermute(x, "head", pairs)

    def across_cores(x):
        return lax.ppermute(x, "head", [(i, i ^ 1) for i in range(8)])

    def swaps(x, along):
        got = []
        for swap in ((3, 2, 1, 0), (1, 0, 3, 2), (2, 3, 0, 1)):
            if along == "x":
                pairs = [(4 * y + i, 4 * y + swap[i]) for y in range(4) for i in range(4)]
            else:
                pairs = [(4 * i + c, 4 * swap[i] + c) for i in range(4) for c in range(4)]
            got.append(lax.ppermute(x, "ctx", pairs))
        return got

    gains = jnp.broadcast_to(norm_gain[:, :, None], (heads, dh, CH))
    message = jnp.einsum("hse,hsd->hed", v, k, preferred_element_type=F32).astype(BF16)
    w_other = across_cores(out_weight)
    parts = [(0, 1, 2), (3, 4)]
    sibs, accs = [], []
    for step, along in enumerate("xy"):
        got = swaps(message, along)
        tied, _ = lax.optimization_barrier((w, message))
        acc = local_part(q, k, v, tied, parts[step], (out_weight,) if step else ())
        low, near, far, acc = lax.optimization_barrier((*got, acc))
        far, low = far.astype(F32), low.astype(F32)
        sibs += [near, (far + low).astype(BF16)]
        accs.append(acc)
        if not step:
            near, w_other = lax.optimization_barrier((near, w_other))
            message = (message.astype(F32) + near.astype(F32) + (far + low)).astype(BF16)

    send1 = far_part(accs, parts, q, w, sibs, gains, 1, (2,))
    other1 = across_cores(send1)
    own1 = far_part(accs, parts, q, w, sibs, gains, 0, (2,))
    (early,) = project([(own1, 0, out_weight)], 0, (width,), (), F32)
    first_up, first_down = project([(other1, 0, w_other)], 0, (split, rest), ((early, 0),))
    late_q, first_up, first_down = lax.optimization_barrier((q, first_up, first_down))
    relay_up = along_z(first_up, 1)
    relay_down = along_z(first_down, -1)
    send2 = far_part(accs, parts, late_q, w, sibs, gains, 1, (1, 3, 0))
    other2 = across_cores(send2)
    own2 = far_part(accs, parts, late_q, w, sibs, gains, 0, (1, 3, 0), FAR_FLOPS)

    def block(i):
        return [(own2, i, out_weight), (other2, i, w_other)]

    direct_up = along_z(project(block(0), split, (rest,))[0], 1)
    direct_down = along_z(project(block(1), 0, (rest,))[0], -1)
    last = width // 20
    up_b, up_a = project(block(0), 0, (last, split - last), ((relay_up, 0),))
    down_a, down_b = project(block(1), rest, (split - last, last), ((relay_down, split - rest),))
    up_a, down_a = along_z(up_a, 1), along_z(down_a, -1)
    up_b, down_b = along_z(up_b, 1), along_z(down_b, -1)
    (mine,) = project(block(2), 0, (width,), ((direct_down, 0), (direct_up, split)), F32, MINE_FLOPS)
    out = finish(mine, [(up_a, last), (down_a, rest)])
    return finish(mine, [(up_b, 0), (down_b, width - last)], out)


def solution(mesh):
    placed = (
        P("ctx", "head", None),
        P("ctx", "head", None),
        P("ctx", "head", None),
        P("ctx", "head", None),
        P("head", None),
        P("head", None),
    )
    return jax.shard_map(
        on_device, mesh=mesh, in_specs=placed, out_specs=P(("ctx", "head"), None), check_vma=False
    )
```
